32 devices in a mesh: grp: 2 (over y), blk: 4 (over z), tile: 4 (over x, core).
Axes of the slice: x: 2, y: 2, z: 4, core: 2. Of those that a mesh axis runs over, the one named last changes fastest.
Arguments:
- fp_values: bfloat16 [6144, 128], P(('grp', 'blk', 'tile')), parts along dimension 0, may hold values from -0.625 to 0.625
- block_owner: int32 [6144], P(('grp', 'blk', 'tile')), parts along dimension 0, may hold values from 0 to 3, as said below
- block_obs: int32 [6144], P(('grp', 'blk', 'tile')), parts along dimension 0, may hold values from 0 to 127
- block_base: int32 [6144], P(('grp', 'blk', 'tile')), parts along dimension 0, may hold values from 0 to 64
- block_count: int32 [6144], P(('grp', 'blk', 'tile')), parts along dimension 0, may hold values from 32 to 128, as said below
- cover_index: int32 [2, 128], replicated, may hold values from 0 to 191
- cover_weight: float32 [2, 128], replicated, may hold values from 0.25 to 1
- spatial_cov: bfloat16 [2048, 1024], P(('grp', 'blk'), 'tile'), parts along dimension 0, as said below
- temporal_cov: float32 [104, 52], P('grp'), parts along dimension 0, as said below
- obs_week: int32 [1024], P('grp'), parts along dimension 0, may hold values from 0 to 51
- obs_error: float32 [1024], P(('grp', 'blk')), parts along dimension 0, may hold values from 0.2 to 1
Outputs:
- panel: float32 [1024, 128], P(('grp', 'blk')), parts along dimension 0
- trailing: float32 [1024, 512], P(('grp', 'blk'), 'tile'), parts along dimension 0
The draws below stay inside these ranges and needn't reach their ends.
There are 2 independent parts, one for each index of `grp`. The reference program is written for one: setup_inputs(seed, part) draws one part's arguments, and reference() takes and returns one part's arrays. A program takes and returns all parts, laid end to end along the dimension named above; an argument that names none is the same for every part. Nothing has to cross between parts.
Inputs may be any that keep to these rules, and one draw needn't show every extreme that they name: `block_owner`: no tile is named by more than 64 of one device's 192 blocks; in every observation block one tile is named by exactly 64 blocks of each of its devices. `block_count`: each device holds at least one block with all cells valid. `spatial_cov`: symmetric positive definite. `temporal_cov`: symmetric positive definite.
All inputs are finite; a program needn't handle non-finite values.
Results may differ from the reference program's by a relative error of at most 0.0033.
Values may be sent and summed in bfloat16 or wider, within the bound.
No kernel may reach another device: no remote copies, remote signals or barrier semaphores. Data moves between devices by JAX's collectives and lax.ppermute only.
A program may use at most 64 MiB of HBM per device.

```python
import math
import jax
import jax.numpy as jnp
from jax import lax

OBS_DEV = 128
CELL_TILE = 256
WEEKS = 52
BLOCK_CELLS = 128
PATCH_SPAN = 192
NOBS = 512
NCELL = 1024
PANEL = 128
BLK_DEV = 192
NBLOCKS = 3072
N_BLK = 4
N_TILE = 4


def shuffle_row(row_key, values):
    order = jax.random.permutation(row_key, values.shape[0])
    return values[order]


def draw_block_owner(key, part):
    devices = N_BLK * N_TILE
    capacity = BLK_DEV // 3
    hot_key = jax.random.fold_in(key, 11)
    shift_key = jax.random.fold_in(key, 12)
    order_key = jax.random.fold_in(key, 13)
    hot_tile = jax.random.randint(hot_key, (N_BLK,), 0, N_TILE)
    hot_device = jnp.repeat(hot_tile, N_TILE)
    shifts = jax.random.randint(shift_key, (devices,), 0, N_TILE - 1)
    slot_ids = jnp.arange(BLK_DEV, dtype=jnp.int32)
    others = (shifts[:, None] + slot_ids[None, :] - capacity) % (N_TILE - 1)
    others = others + (others >= hot_device[:, None]).astype(jnp.int32)
    owners = jnp.where(slot_ids[None, :] < capacity, hot_device[:, None], others)
    row_keys = jax.random.split(order_key, devices)
    owners = jax.vmap(shuffle_row)(row_keys, owners)
    return owners.reshape(-1).astype(jnp.int32)


def draw_block_count(key, part):
    devices = N_BLK * N_TILE
    count_key = jax.random.fold_in(key, 21)
    full_key = jax.random.fold_in(key, 22)
    counts = jax.random.randint(count_key, (devices, BLK_DEV), BLOCK_CELLS // 4, BLOCK_CELLS + 1)
    full_slot = jax.random.randint(full_key, (devices,), 0, BLK_DEV)
    counts = counts.at[jnp.arange(devices), full_slot].set(BLOCK_CELLS)
    return counts.reshape(-1).astype(jnp.int32)


def draw_spatial_cov(key, part):
    place_key = jax.random.fold_in(key, 31)
    scale_key = jax.random.fold_in(key, 32)
    nugget_key = jax.random.fold_in(key, 33)
    places = jax.random.uniform(place_key, (NCELL, 2), jnp.float32)
    scales = jnp.exp(jax.random.uniform(scale_key, (NCELL,), jnp.float32, jnp.log(0.5), jnp.log(2.0)))
    length = 0.15
    apart = places[:, None, :] - places[None, :, :]
    distance = jnp.sqrt(jnp.sum(apart * apart, axis=2))
    nugget = jax.random.uniform(nugget_key, (NCELL,), jnp.float32, 0.1, 0.4)
    cov = scales[:, None] * scales[None, :] * jnp.exp(-distance / length) + jnp.diag(nugget)
    return cov.astype(jnp.bfloat16)


def draw_temporal_cov(key, part):
    scale_key = jax.random.fold_in(key, 41)
    length_key = jax.random.fold_in(key, 42)
    nugget_key = jax.random.fold_in(key, 43)
    scales = jnp.exp(jax.random.uniform(scale_key, (WEEKS,), jnp.float32, jnp.log(0.6), jnp.log(1.6)))
    length = jax.random.uniform(length_key, (), jnp.float32, 1.5, 6.0)
    weeks = jnp.arange(WEEKS, dtype=jnp.float32)
    lags = jnp.abs(weeks[:, None] - weeks[None, :])
    nugget = jax.random.uniform(nugget_key, (WEEKS,), jnp.float32, 0.05, 0.2)
    return scales[:, None] * scales[None, :] * jnp.exp(-lags / length) + jnp.diag(nugget)


def with_ends(values, own_key, low, top_value):
    dims = values.shape
    place = [jax.random.randint(jax.random.fold_in(own_key, axis), (), 0, dims[axis]) for axis in range(len(dims))]
    values = values.at[tuple(place)].set(low)
    longest = dims.index(max(dims))
    place[longest] = (place[longest] + 1) % dims[longest]
    return values.at[tuple(place)].set(top_value)


def block_scale(stream_key, dims, pieces, least, largest):
    def one(position, blocks):
        draws = jax.random.uniform(jax.random.fold_in(jax.random.fold_in(stream_key, 6), position), (blocks,), jnp.float32, least / len(pieces), largest / len(pieces))
        return jnp.repeat(jnp.exp(draws), dims[position] // blocks).reshape((-1,) + (1,) * (len(dims) - position - 1))

    level = one(*pieces[0])
    for cut in pieces[1:]:
        level = level * one(*cut)
    return level


def noise(rng, extent, scale, limit, shards=(), kind=jnp.bfloat16):
    factor_of = block_scale(rng, extent, shards, -0.22, 0.18) if shards else 1.0
    values = jax.random.normal(rng, extent, jnp.float32) * scale * factor_of
    return jnp.minimum(jnp.maximum(values, -limit), limit).astype(kind)


def setup_inputs(seed: int = 0, part: int = 0) -> dict:
    arg_keys = jax.random.split(jax.random.key(seed), 12)
    own_keys = jax.random.split(jax.random.fold_in(arg_keys[11], part), 12)
    fp_values = noise(own_keys[0], (NBLOCKS, BLOCK_CELLS), 0.045, 0.625, ((0, 16),))
    block_owner = draw_block_owner(jax.random.fold_in(jax.random.fold_in(arg_keys[11], part), 71), part)
    block_obs = with_ends(jax.random.randint(own_keys[2], (NBLOCKS,), 0, OBS_DEV), jax.random.fold_in(own_keys[2], 1), 0, OBS_DEV - 1).astype(jnp.int32)
    block_base = with_ends(jax.random.randint(own_keys[3], (NBLOCKS,), 0, CELL_TILE - PATCH_SPAN + 1), jax.random.fold_in(own_keys[3], 1), 0, CELL_TILE - PATCH_SPAN).astype(jnp.int32)
    block_count = draw_block_count(jax.random.fold_in(jax.random.fold_in(arg_keys[11], part), 71), part)
    cover_index = with_ends(jax.random.randint(arg_keys[5], (2, BLOCK_CELLS), 0, PATCH_SPAN), jax.random.fold_in(arg_keys[5], 1), 0, PATCH_SPAN - 1).astype(jnp.int32)
    cover_weight = jnp.clip(jax.random.uniform(arg_keys[6], (2, BLOCK_CELLS), jnp.float32, 0.25, 1.0), 0.25, 1.0)
    spatial_cov = draw_spatial_cov(jax.random.fold_in(jax.random.fold_in(arg_keys[11], part), 71), part)
    temporal_cov = draw_temporal_cov(jax.random.fold_in(jax.random.fold_in(arg_keys[11], part), 71), part)
    obs_week = with_ends(jax.random.randint(own_keys[9], (NOBS,), 0, WEEKS), jax.random.fold_in(own_keys[9], 1), 0, WEEKS - 1).astype(jnp.int32)
    obs_error = jnp.clip(jnp.exp(math.log(1.0) - 1.609438 * jax.random.uniform(own_keys[10], (NOBS,), jnp.float32) ** block_scale(own_keys[10], (NOBS,), ((0, 4),), -0.2, 0.2)), 0.2, 1.0)
    return dict(fp_values=fp_values, block_owner=block_owner, block_obs=block_obs, block_base=block_base, block_count=block_count, cover_index=cover_index, cover_weight=cover_weight, spatial_cov=spatial_cov, temporal_cov=temporal_cov, obs_week=obs_week, obs_error=obs_error)


def reference(fp_values, block_owner, block_obs, block_base, block_count, cover_index, cover_weight, spatial_cov, temporal_cov, obs_week, obs_error):
    block_total = fp_values.shape[0]
    cell_ids = jnp.arange(BLOCK_CELLS, dtype=jnp.int32)
    kept = jnp.where(cell_ids[None, :] < block_count[:, None], fp_values, jnp.zeros_like(fp_values))
    row_block = (jnp.arange(block_total, dtype=jnp.int32) // (N_TILE * BLK_DEV)).astype(jnp.int32)
    rows = row_block * OBS_DEV + block_obs
    columns = block_owner[:, None, None] * CELL_TILE + block_base[:, None, None] + cover_index[None, :, :]
    row_index = jnp.broadcast_to(rows[:, None, None], columns.shape)
    contrib = kept.astype(jnp.float32)[:, None, :] * cover_weight[None, :, :]
    dense = jnp.zeros((NOBS, NCELL), jnp.float32).at[row_index, columns].add(contrib)
    footprints = dense.astype(jnp.bfloat16)
    product = jnp.dot(footprints.astype(jnp.float32), spatial_cov.astype(jnp.float32), preferred_element_type=jnp.float32).astype(jnp.bfloat16)
    pairs = jnp.dot(product.astype(jnp.float32), footprints.T.astype(jnp.float32), preferred_element_type=jnp.float32)
    week_cov = temporal_cov[obs_week][:, obs_week]
    innovation = pairs * week_cov + jnp.diag(obs_error)
    top = innovation[:PANEL, :PANEL]
    pivot = jnp.linalg.cholesky(0.5 * (top + top.T))
    panel = jax.scipy.linalg.solve_triangular(pivot, innovation[:, :PANEL].T, lower=True).T
    column_factor = jax.scipy.linalg.solve_triangular(pivot, innovation[:PANEL, :], lower=True).T
    trailing = innovation - jnp.dot(panel, column_factor.T, precision=lax.Precision.HIGHEST)
    return (panel, trailing)
```

```python
import functools

import jax
import jax.numpy as jnp
from jax import lax
from jax.experimental import pallas as pl
from jax.experimental.pallas import tpu as pltpu
from jax.sharding import PartitionSpec as P

PANEL_MAX = 128
LANES = 128
BASE_BITS = 7
INDEX_ROWS = 16
HIGHEST = lax.Precision.HIGHEST
BF16 = jnp.bfloat16
F32 = jnp.float32
CONTRACT_LAST = (((1,), (1,)), ((), ()))
CONTRACT_FIRST = (((0,), (0,)), ((), ()))


def split_rows(row):
    width = row.shape[1]
    pieces = []
    for start in range(0, width, LANES):
        piece = row[:, start : min(start + LANES, width)]
        if piece.shape[1] < LANES:
            pad = jnp.zeros((1, LANES - piece.shape[1]), row.dtype)
            piece = jnp.concatenate([piece, pad], axis=1)
        pieces.append(piece)
    return pieces


def three_parts(value):
    high = value.astype(BF16).astype(F32)
    rest = value - high
    middle = rest.astype(BF16).astype(F32)
    return high, middle, rest - middle


def pack_kernel(values_ref, obs_ref, base_ref, owner_ref, count_ref, error_ref, out_ref):
    slots, cells = values_ref.shape
    count = jnp.transpose(jnp.broadcast_to(count_ref[...].astype(F32), (cells, slots)))
    cell = lax.broadcasted_iota(jnp.int32, (slots, cells), 1).astype(F32)
    values = values_ref[...].astype(F32)
    out_ref[0:slots, :] = jnp.where(cell < count, values, 0.0).astype(BF16)
    rows = []
    for ref in (obs_ref, base_ref, owner_ref):
        rows += split_rows(ref[...].astype(F32))
    rows += list(three_parts(error_ref[...]))
    place = lax.broadcasted_iota(jnp.int32, (INDEX_ROWS, LANES), 0)
    tail = jnp.zeros((INDEX_ROWS, LANES), F32)
    for index, row in enumerate(rows):
        tail = jnp.where(place == index, jnp.broadcast_to(row, tail.shape), tail)
    out_ref[slots:, :] = tail.astype(BF16)


def join_rows(tail, first, width):
    pieces = []
    for number, start in enumerate(range(0, width, LANES)):
        row = tail[first + number : first + number + 1, :]
        pieces.append(row[:, 0 : min(LANES, width - start)])
    return pieces[0] if len(pieces) == 1 else jnp.concatenate(pieces, axis=1)


def cover_parts(index_ref, weight_ref, cell_tile):
    covers, cells = index_ref.shape
    column = lax.broadcasted_iota(jnp.int32, (cell_tile, cells), 0)
    total = jnp.zeros((cell_tile, cells), F32)
    for cover in range(covers):
        hit = column == index_ref[cover : cover + 1, :]
        total = total + jnp.where(hit, weight_ref[cover : cover + 1, :], 0.0)
    high = total.astype(BF16)
    low = (total - high.astype(F32)).astype(BF16)
    return jnp.concatenate([high, low], axis=1)


def regrid_kernel(n_tile, slots, obs_rows, cell_tile, raw_ref, index_ref, weight_ref, out_ref, sum_ref):
    cover = cover_parts(index_ref, weight_ref, cell_tile)
    count_rows = -(-slots // LANES)
    step = slots + INDEX_ROWS
    sets = raw_ref.shape[0] // (n_tile * step)
    for part in range(sets):
        for tile in range(n_tile):
            start = (tile * sets + part) * step
            kept = raw_ref[start : start + slots, :]
            tail = raw_ref[start + slots : start + step, :].astype(F32)
            obs = join_rows(tail, 0, slots)
            base = join_rows(tail, count_rows, slots)
            owner = join_rows(tail, 2 * count_rows, slots)
            patch = lax.dot_general(
                jnp.concatenate([kept, kept], axis=1), cover, CONTRACT_LAST, preferred_element_type=F32
            )
            shift = jnp.transpose(jnp.broadcast_to(base, (LANES, slots))).astype(jnp.int32)
            shift = jnp.concatenate([shift] * (cell_tile // LANES), axis=1)
            for bit in range(BASE_BITS):
                moved = pltpu.roll(patch, 1 << bit, axis=1)
                patch = jnp.where((shift & (1 << bit)) != 0, moved, patch)
            high = patch.astype(BF16)
            low = (patch - high.astype(F32)).astype(BF16)
            key = owner * obs_rows + obs
            row = lax.broadcasted_iota(jnp.int32, (n_tile * obs_rows, slots), 0).astype(F32)
            onehot = jnp.where(row == key, 1.0, 0.0).astype(BF16)
            both = jnp.concatenate([high, low], axis=1)
            term = jnp.dot(onehot, both, preferred_element_type=F32)
            term = term[:, 0:cell_tile] + term[:, cell_tile:]
            if tile == 0:
                sum_ref[...] = term
            else:
                sum_ref[...] += term
        for tile in range(n_tile):
            rows = sum_ref[tile * obs_rows : (tile + 1) * obs_rows, :]
            out_ref[part * obs_rows : (part + 1) * obs_rows, tile * cell_tile : (tile + 1) * cell_tile] = (
                rows.astype(BF16)
            )


def product_kernel(place_ref, prints_ref, *refs):
    cov_refs, out_ref = refs[:-1], refs[-1]
    depth = cov_refs[0].shape[0]
    total = None
    for number, cov_ref in enumerate(cov_refs):
        start = pl.multiple_of(place_ref[number] * depth, depth)
        term = jnp.dot(prints_ref[:, pl.ds(start, depth)], cov_ref[...], preferred_element_type=F32)
        total = term if total is None else total + term
    out_ref[...] = total.astype(BF16)


def week_kernel(obs_rows, width, place_ref, week_ref, cov_ref, out_ref):
    weeks = cov_ref.shape[0]
    row_start = pl.multiple_of(place_ref[0] * obs_rows, obs_rows)
    col_start = pl.multiple_of(place_ref[1] * width, width)
    head = week_ref[:, 0:obs_rows]
    mine = week_ref[:, pl.ds(row_start, obs_rows)]
    cols = week_ref[:, pl.ds(col_start, width)]

    def onehot(row):
        week = lax.broadcasted_iota(jnp.int32, (weeks, row.shape[1]), 0)
        return jnp.where(week == row, 1.0, 0.0)

    rows = onehot(jnp.concatenate([mine, head], axis=1))
    picked = jnp.dot(
        cov_ref[...], onehot(jnp.concatenate([head, cols], axis=1)), precision=HIGHEST, preferred_element_type=F32
    )
    out_ref[...] = lax.dot_general(rows, picked, CONTRACT_FIRST, precision=HIGHEST, preferred_element_type=F32)


def inverse_factor(matrix):
    size = matrix.shape[0]
    groups = size // 8
    left = [matrix[8 * g : 8 * g + 8, :] for g in range(groups)]
    sub = lax.broadcasted_iota(jnp.int32, (8, size), 0)
    lane = lax.broadcasted_iota(jnp.int32, (8, size), 1)
    right = [jnp.where(sub + 8 * g == lane, 1.0, 0.0) for g in range(groups)]
    scale = [jnp.zeros((8, 1), F32) for _ in range(groups)]
    sub_column = lax.broadcasted_iota(jnp.int32, (8, 1), 0)
    for k in range(size):
        g, s = divmod(k, 8)
        row = left[g][s : s + 1, :]
        mirror = right[g][s : s + 1, :]
        pivot = row[:, k : k + 1]
        scale[g] = jnp.where(sub_column == s, pivot, scale[g])
        inverse = 1.0 / pivot
        row = row * inverse
        mirror = mirror * inverse
        for h in range(g, groups):
            column = left[h][:, k : k + 1]
            if h == g:
                column = jnp.where(sub_column > s, column, 0.0)
            left[h] = left[h] - column * row
            right[h] = right[h] - column * mirror
    return jnp.concatenate([right[g] * lax.rsqrt(scale[g]) for g in range(groups)], axis=0)


def place_diagonal(row):
    size = row.shape[1]
    sub = lax.broadcasted_iota(jnp.int32, (size, size), 0)
    lane = lax.broadcasted_iota(jnp.int32, (size, size), 1)
    return jnp.where(sub == lane, jnp.broadcast_to(row, (size, size)), 0.0)


def pair_terms(n_tile, product_ref, prints, cell_tile):
    rows = product_ref.shape[0] // n_tile
    total = None
    for tile in range(n_tile):
        term = lax.dot_general(
            product_ref[tile * rows : (tile + 1) * rows, :],
            prints[:, tile * cell_tile : (tile + 1) * cell_tile],
            CONTRACT_LAST,
            preferred_element_type=F32,
        )
        total = term if total is None else total + term
    return total


def factor_kernel(n_tile, panel_width, place_ref, product_ref, prints_ref, week_ref, raw_ref, panel_ref, inverse_ref):
    cell_tile = product_ref.shape[1]
    obs_rows = panel_ref.shape[0]
    prints = prints_ref[obs_rows : obs_rows + panel_width, :]
    pairs = pair_terms(n_tile, product_ref, prints, cell_tile)
    scaled = pairs * week_ref[:, 0:panel_width]
    parts = raw_ref[...].astype(F32)
    error = jnp.sum(parts, axis=0, keepdims=True)
    diagonal = place_diagonal(error)
    top = scaled[obs_rows:, :] + diagonal
    mine = scaled[0:obs_rows, :] + jnp.where(place_ref[0] == 0, 1.0, 0.0) * diagonal
    inverse = inverse_factor(0.5 * (top + jnp.transpose(top)))
    inverse_ref[...] = inverse
    panel_ref[...] = lax.dot_general(mine, inverse, CONTRACT_LAST, precision=HIGHEST, preferred_element_type=F32)


def trail_kernel(
    n_tile, panel_width, place_ref, product_ref, week_ref, error_ref, head_ref, panel_ref, inverse_ref, prints_ref, *refs
):
    print_refs, out_ref = refs[:-1], refs[-1]
    obs_rows, width = out_ref.shape
    cell_tile = product_ref.shape[1]
    own = jnp.where(place_ref[0] == place_ref[1], 1.0, 0.0).astype(BF16)
    prints = prints_ref[...] * own
    for ref in print_refs:
        prints = prints + ref[...]
    pairs = pair_terms(n_tile, product_ref, prints, cell_tile)
    scaled = pairs * week_ref[:, panel_width:]
    sub = lax.broadcasted_iota(jnp.int32, (obs_rows, width), 0) + place_ref[0] * obs_rows
    lane = lax.broadcasted_iota(jnp.int32, (obs_rows, width), 1) + place_ref[1] * width
    top_sub = lax.broadcasted_iota(jnp.int32, (obs_rows, width), 0)
    repeat = width // obs_rows
    error = jnp.concatenate([error_ref[...]] * repeat, axis=1)
    head = jnp.concatenate([jnp.sum(head_ref[...].astype(F32), axis=0, keepdims=True)] * repeat, axis=1)
    mine = scaled[0:obs_rows, :] + jnp.where(sub == lane, error, 0.0)
    top = scaled[obs_rows:, :] + jnp.where(top_sub == lane, head, 0.0)
    factor = jnp.dot(inverse_ref[...], top, precision=HIGHEST, preferred_element_type=F32)
    out_ref[...] = mine - jnp.dot(panel_ref[...], factor, precision=HIGHEST, preferred_element_type=F32)


def ring(size, shift):
    return [(i, (i + shift) % size) for i in range(size)]


def smem():
    return pl.BlockSpec(memory_space=pltpu.SMEM)


def vmem():
    return pl.BlockSpec(memory_space=pltpu.VMEM)


def call(kernel, out, count, scalars=0, scratch=(), name=None):
    return pl.pallas_call(
        kernel,
        out_shape=out,
        in_specs=[smem()] * scalars + [vmem()] * (count - scalars),
        out_specs=jax.tree.map(lambda _: vmem(), out),
        scratch_shapes=list(scratch),
        name=name,
    )


def body(
    fp_values,
    block_owner,
    block_obs,
    block_base,
    block_count,
    cover_index,
    cover_weight,
    spatial_cov,
    temporal_cov,
    obs_week,
    obs_error,
):
    n_tile = lax.axis_size("tile")
    n_blk = lax.axis_size("blk")
    tile_rank = lax.axis_index("tile").astype(jnp.int32)
    blk_rank = lax.axis_index("blk").astype(jnp.int32)
    cell_tile = spatial_cov.shape[1]
    slots, cells = fp_values.shape
    obs_rows = obs_error.shape[0]
    all_cells = cell_tile * n_tile
    width = obs_rows * n_blk // n_tile
    panel_width = min(PANEL_MAX, width)
    place = jnp.stack([blk_rank, tile_rank])
    square = n_blk == n_tile

    rows = slots + INDEX_ROWS
    packed = call(pack_kernel, jax.ShapeDtypeStruct((rows, cells), BF16), 6, name="pack")(
        fp_values,
        block_obs.reshape(1, slots),
        block_base.reshape(1, slots),
        block_owner.reshape(1, slots),
        block_count.reshape(1, slots),
        obs_error.reshape(1, obs_rows),
    )
    reach = 1
    head = packed
    if n_blk <= 4:
        got = [lax.ppermute(packed, "blk", [(0, s)]) for s in range(1, n_blk)]
        total = functools.reduce(jnp.add, got)
        head = jnp.where(blk_rank == 0, packed, total)
    else:
        while reach < n_blk:
            pairs = [(i, i + reach) for i in range(reach) if i + reach < n_blk]
            got = lax.ppermute(head, "blk", pairs)
            fresh = (blk_rank >= reach) & (blk_rank < 2 * reach)
            head = jnp.where(fresh, got, head)
            reach *= 2
    if n_blk <= 4:
        covs = [spatial_cov] + [lax.ppermute(spatial_cov, "blk", ring(n_blk, s)) for s in range(1, n_blk)]
        sources = jnp.stack([(blk_rank - s) % n_blk for s in range(n_blk)])
    else:
        covs = [lax.all_gather(spatial_cov, "blk", axis=0, tiled=True)]
        sources = jnp.zeros((1,), jnp.int32)
    raw = lax.all_gather(jnp.concatenate([packed, head], axis=0), "tile", axis=0, tiled=True)
    prints = call(
        functools.partial(regrid_kernel, n_tile, slots, obs_rows, cell_tile),
        jax.ShapeDtypeStruct((2 * obs_rows, all_cells), BF16),
        3,
        scratch=[pltpu.VMEM((n_tile * obs_rows, cell_tile), F32)],
        name="regrid",
    )(raw, cover_index, cover_weight)
    week_cov = call(
        functools.partial(week_kernel, obs_rows, width),
        jax.ShapeDtypeStruct((2 * obs_rows, panel_width + width), F32),
        3,
        1,
        name="week",
    )(place, obs_week.reshape(1, -1), temporal_cov)
    mine = prints[0:obs_rows, :]
    if square:
        others = []
        for s in range(1, n_blk):
            pairs = [(t * n_tile + t, ((t + s) % n_blk) * n_tile + t) for t in range(n_tile)]
            others.append(lax.ppermute(mine, ("blk", "tile"), pairs))
    else:
        own = lax.dynamic_slice_in_dim(mine, tile_rank * cell_tile, cell_tile, axis=1)
        every = lax.all_gather(own, "blk", axis=0, tiled=True)
        spread = lax.all_to_all(every, "tile", 0, 0, tiled=True)
        spread = spread.reshape(n_tile, width, cell_tile)
        others = [jnp.swapaxes(spread, 0, 1).reshape(width, all_cells)]
    product = call(
        product_kernel, jax.ShapeDtypeStruct((2 * obs_rows, cell_tile), BF16), 2 + len(covs), 1, name="product"
    )(sources, prints, *covs)
    products = lax.all_gather(product, "tile", axis=0, tiled=True)
    first = slots + 3 * (-(-slots // LANES))
    head_parts = head[first : first + 3, :]
    panel, inverse = call(
        functools.partial(factor_kernel, n_tile, panel_width),
        (
            jax.ShapeDtypeStruct((obs_rows, panel_width), F32),
            jax.ShapeDtypeStruct((panel_width, panel_width), F32),
        ),
        5,
        1,
        name="factor",
    )(place, products, prints, week_cov, head_parts)
    trail_place = place if square else jnp.stack([blk_rank, tile_rank, jnp.zeros((), jnp.int32)])
    own_prints = mine if square else jnp.zeros((width, all_cells), BF16)
    trailing = call(
        functools.partial(trail_kernel, n_tile, panel_width),
        jax.ShapeDtypeStruct((obs_rows, width), F32),
        8 + len(others),
        1,
        name="trail",
    )(trail_place, products, week_cov, obs_error.reshape(1, obs_rows), head_parts, panel, inverse, own_prints, *others)
    return panel, trailing


def solution(mesh):
    placed = (
        P(("grp", "blk", "tile"), None),
        P(("grp", "blk", "tile")),
        P(("grp", "blk", "tile")),
        P(("grp", "blk", "tile")),
        P(("grp", "blk", "tile")),
        P(),
        P(),
        P(("grp", "blk"), "tile"),
        P("grp", None),
        P("grp"),
        P(("grp", "blk")),
    )
    return jax.shard_map(
        body,
        mesh=mesh,
        in_specs=placed,
        out_specs=(P(("grp", "blk"), None), P(("grp", "blk"), "tile")),
        check_vma=False,
    )
```

```python
import functools

import jax
import jax.numpy as jnp
from jax import lax
from jax.experimental import pallas as pl
from jax.experimental.pallas import tpu as pltpu
from jax.sharding import PartitionSpec as P

PANEL_MAX = 128
LANES = 128
INDEX_ROWS = 16
DIRECT_MAX = 4
HIGHEST = lax.Precision.HIGHEST
BF16 = jnp.bfloat16
F32 = jnp.float32
I32 = jnp.int32
CONTRACT_LAST = (((1,), (1,)), ((), ()))
CONTRACT_FIRST = (((0,), (0,)), ((), ()))


def rank(axis):
    return lax.axis_index(axis).astype(I32)


def direct(axis_size):
    return axis_size <= DIRECT_MAX


def slot_of(wanted, own, axis_size):
    return own ^ wanted if direct(axis_size) else wanted


def split_rows(row):
    width = row.shape[1]
    pieces = []
    for start in range(0, width, LANES):
        piece = row[:, start : min(start + LANES, width)]
        if piece.shape[1] < LANES:
            pad = jnp.zeros((1, LANES - piece.shape[1]), row.dtype)
            piece = jnp.concatenate([piece, pad], axis=1)
        pieces.append(piece)
    return pieces


def three_parts(value):
    high = value.astype(BF16).astype(F32)
    rest = value - high
    middle = rest.astype(BF16).astype(F32)
    return high, middle, rest - middle


def pack_kernel(values_ref, obs_ref, base_ref, owner_ref, count_ref, error_ref, out_ref):
    slots, cells = values_ref.shape
    count = jnp.transpose(jnp.broadcast_to(count_ref[...].astype(F32), (cells, slots)))
    cell = lax.broadcasted_iota(I32, (slots, cells), 1).astype(F32)
    values = values_ref[...].astype(F32)
    out_ref[0:slots, :] = jnp.where(cell < count, values, 0.0).astype(BF16)
    rows = []
    for ref in (obs_ref, base_ref, owner_ref):
        rows += split_rows(ref[...].astype(F32))
    rows += list(three_parts(error_ref[...]))
    place = lax.broadcasted_iota(I32, (INDEX_ROWS, LANES), 0)
    tail = jnp.zeros((INDEX_ROWS, LANES), F32)
    for index, row in enumerate(rows):
        tail = jnp.where(place == index, jnp.broadcast_to(row, tail.shape), tail)
    out_ref[slots:, :] = tail.astype(BF16)


def join_rows(tail, first, width):
    pieces = []
    for number, start in enumerate(range(0, width, LANES)):
        row = tail[first + number : first + number + 1, :]
        pieces.append(row[:, 0 : min(LANES, width - start)])
    return pieces[0] if len(pieces) == 1 else jnp.concatenate(pieces, axis=1)


def cover_parts(index_ref, weight_ref, cell_tile):
    covers, cells = index_ref.shape
    column = lax.broadcasted_iota(I32, (cell_tile, cells), 0)
    total = jnp.zeros((cell_tile, cells), F32)
    for cover in range(covers):
        hit = column == index_ref[cover : cover + 1, :]
        total = total + jnp.where(hit, weight_ref[cover : cover + 1, :], 0.0)
    high = total.astype(BF16)
    low = (total - high.astype(F32)).astype(BF16)
    return jnp.concatenate([high, low], axis=1)


def regrid(raw_ref, slot, cover, slots, obs_rows):
    n_tile = raw_ref.shape[0]
    cell_tile = cover.shape[0]
    count_rows = -(-slots // LANES)
    lane = lax.broadcasted_iota(I32, (slots, LANES), 1)
    highs, lows, owners, obses = [], [], [], []
    for tile in range(n_tile):
        block = raw_ref.at[tile, slot]
        kept = block[0:slots, :]
        tail = block[slots : slots + INDEX_ROWS, :].astype(F32)
        obses.append(join_rows(tail, 0, slots))
        base = join_rows(tail, count_rows, slots)
        owners.append(join_rows(tail, 2 * count_rows, slots))
        patch = lax.dot_general(
            jnp.concatenate([kept, kept], axis=1), cover, CONTRACT_LAST, preferred_element_type=F32
        )
        shift = jnp.transpose(jnp.broadcast_to(base, (LANES, slots))).astype(I32)
        source = (lane - shift) & (LANES - 1)
        inside = lane >= shift
        moved = []
        before = jnp.zeros((slots, LANES), F32)
        for start in range(0, cell_tile, LANES):
            turned = jnp.take_along_axis(patch[:, start : start + LANES], source, axis=1)
            moved.append(jnp.where(inside, turned, before))
            before = turned
        patch = jnp.concatenate(moved, axis=1)
        high = patch.astype(BF16)
        highs.append(high)
        lows.append((patch - high.astype(F32)).astype(BF16))
    owner = jnp.concatenate(owners, axis=1)
    obs = jnp.concatenate(obses, axis=1)
    row = lax.broadcasted_iota(I32, (obs_rows, owner.shape[1]), 0).astype(F32).astype(BF16)
    one, zero = jnp.ones((), BF16), jnp.zeros((), BF16)
    hits = []
    for tile in range(n_tile):
        key = jnp.where(owner == tile, obs, -1.0).astype(BF16)
        hits.append(jnp.where(row == key, one, zero))
    hits = jnp.concatenate(hits, axis=0)
    total = jnp.dot(
        jnp.concatenate([hits, hits], axis=1), jnp.concatenate(highs + lows, axis=0), preferred_element_type=F32
    ).astype(BF16)
    return [total[tile * obs_rows : (tile + 1) * obs_rows, :] for tile in range(n_tile)]


def product_kernel(slots, obs_rows, raw_ref, index_ref, weight_ref, *refs):
    *cov_refs, product_ref, head_ref, error_ref, prints_ref = refs
    cell_tile = product_ref.shape[1]
    n_blk = lax.axis_size("blk")
    me = rank("blk")
    cover = cover_parts(index_ref, weight_ref, cell_tile)
    for part, block in enumerate((me, 0)):
        pieces = regrid(raw_ref, slot_of(block, me, n_blk), cover, slots, obs_rows)
        for tile, piece in enumerate(pieces):
            columns = slice(tile * cell_tile, (tile + 1) * cell_tile)
            prints_ref[part * obs_rows : (part + 1) * obs_rows, columns] = piece
            if part:
                head_ref[:, columns] = piece
    total = None
    for number, cov_ref in enumerate(cov_refs):
        depth = cov_ref.shape[0]
        source = (me ^ number) if len(cov_refs) > 1 else 0
        start = pl.multiple_of(source * depth, min(depth, LANES))
        term = jnp.dot(prints_ref[:, pl.ds(start, depth)], cov_ref[...], preferred_element_type=F32)
        total = term if total is None else total + term
    product_ref[...] = total.astype(BF16)
    first = slots + 3 * (-(-slots // LANES))
    parts = raw_ref.at[0, slot_of(0, me, n_blk)][slots : slots + INDEX_ROWS, :].astype(F32)
    error_ref[...] = jnp.sum(parts[first - slots : first - slots + 3, :], axis=0, keepdims=True)


def column_kernel(slots, obs_rows, panel_width, raw_ref, index_ref, weight_ref, week_ref, cov_ref, prints_ref, out_ref):
    n_blk = lax.axis_size("blk")
    width, all_cells = prints_ref.shape
    cell_tile = all_cells // raw_ref.shape[0]
    me, tile_me = rank("blk"), rank("tile")
    cover = cover_parts(index_ref, weight_ref, cell_tile)
    for part in range(width // obs_rows):
        block = tile_me * (width // obs_rows) + part
        pieces = regrid(raw_ref, slot_of(block, me, n_blk), cover, slots, obs_rows)
        for tile, piece in enumerate(pieces):
            prints_ref[part * obs_rows : (part + 1) * obs_rows, tile * cell_tile : (tile + 1) * cell_tile] = piece
    weeks = cov_ref.shape[0]
    head = week_ref[:, 0:panel_width]
    mine = week_ref[:, pl.ds(pl.multiple_of(me * obs_rows, LANES), obs_rows)]
    cols = week_ref[:, pl.ds(pl.multiple_of(tile_me * width, LANES), width)]

    def onehot(row):
        week = lax.broadcasted_iota(I32, (weeks, row.shape[1]), 0)
        return jnp.where(week == row, 1.0, 0.0)

    rows = onehot(jnp.concatenate([mine, head], axis=1))
    picked = jnp.dot(
        cov_ref[...], onehot(jnp.concatenate([head, cols], axis=1)), precision=HIGHEST, preferred_element_type=F32
    )
    out_ref[...] = lax.dot_general(rows, picked, CONTRACT_FIRST, precision=HIGHEST, preferred_element_type=F32)


def inverse_factor(matrix, out_ref):
    size = matrix.shape[0]
    groups = size // 8
    sub = lax.broadcasted_iota(I32, (8, size), 0)
    lane = lax.broadcasted_iota(I32, (8, size), 1)
    left = [matrix[8 * g : 8 * g + 8, :] for g in range(groups)]
    right = [jnp.where(sub + 8 * g == lane, 1.0, 0.0) for g in range(groups)]

    def spread(block, column):
        return jnp.broadcast_to(block[:, column : column + 1], (8, size))

    for g in range(groups):
        cols = [spread(left[g], 8 * g + m) for m in range(8)]
        a, r = left[g], right[g]
        for i in range(8):
            pivot = cols[i][i : i + 1, :]
            inverse = 1.0 / pivot
            out_ref[8 * g + i : 8 * g + i + 1, :] = r[i : i + 1, :] * lax.rsqrt(pivot)
            here = sub == i
            f = cols[i]
            for m in range(i + 1, 8):
                s = cols[m][i : i + 1, :] * inverse
                cols[m] = jnp.where(here, s, cols[m] - f * s)
            ra = a[i : i + 1, :] * inverse
            rr = r[i : i + 1, :] * inverse
            a = jnp.where(here, ra, a - f * ra)
            r = jnp.where(here, rr, r - f * rr)
        for h in range(g + 1, groups):
            da = dr = None
            for m in range(8):
                c = spread(left[h], 8 * g + m)
                ta = c * a[m : m + 1, :]
                tr = c * r[m : m + 1, :]
                da = ta if da is None else da + ta
                dr = tr if dr is None else dr + tr
            left[h] = left[h] - da
            right[h] = right[h] - dr


def final_kernel(obs_rows, head_ref, prints_ref, week_ref, head_error_ref, error_ref, *refs):
    *product_refs, panel_ref, out_ref, inverse_ref = refs
    panel_width = panel_ref.shape[1]
    width = out_ref.shape[1]
    me, tile_me = rank("blk"), rank("tile")
    tiles = []
    for number, ref in enumerate(product_refs):
        if len(product_refs) > 1:
            tiles.append((tile_me ^ number, ref[...]))
        else:
            rows = 2 * obs_rows
            tiles += [(t, ref[t * rows : (t + 1) * rows, :]) for t in range(ref.shape[0] // rows)]

    def pairs(ref):
        total = None
        for tile, product in tiles:
            cells = product.shape[1]
            start = tile * cells if isinstance(tile, int) else pl.multiple_of(tile * cells, LANES)
            term = lax.dot_general(
                product, ref[:, pl.ds(start, cells)], CONTRACT_LAST, preferred_element_type=F32
            )
            total = term if total is None else total + term
        return total

    head = pairs(head_ref) * week_ref[:, 0:panel_width]
    sub = lax.broadcasted_iota(I32, (obs_rows, panel_width), 0)
    lane = lax.broadcasted_iota(I32, (obs_rows, panel_width), 1)
    diagonal = jnp.where(sub == lane, head_error_ref[...], 0.0)
    top = head[obs_rows:, :] + diagonal
    inverse_factor(0.5 * (top + jnp.transpose(top)), inverse_ref)
    mine = head[0:obs_rows, :] + jnp.where(me == 0, diagonal, 0.0)
    inverse = inverse_ref[...]
    panel = lax.dot_general(mine, inverse, CONTRACT_LAST, precision=HIGHEST, preferred_element_type=F32)
    panel_ref[...] = panel
    rest = pairs(prints_ref) * week_ref[:, panel_width:]
    sub = lax.broadcasted_iota(I32, (obs_rows, width), 0)
    lane = lax.broadcasted_iota(I32, (obs_rows, width), 1) + tile_me * width
    repeat = width // obs_rows
    error = jnp.concatenate([error_ref[...]] * repeat, axis=1)
    head_error = jnp.concatenate([head_error_ref[...]] * repeat, axis=1)
    own = rest[0:obs_rows, :] + jnp.where(sub + me * obs_rows == lane, error, 0.0)
    top = rest[obs_rows:, :] + jnp.where(sub == lane, head_error, 0.0)
    factor = jnp.dot(inverse, top, precision=HIGHEST, preferred_element_type=F32)
    out_ref[...] = own - jnp.dot(panel, factor, precision=HIGHEST, preferred_element_type=F32)


def call(kernel, out, count, scratch=(), name=None):
    spec = pl.BlockSpec(memory_space=pltpu.VMEM)
    return pl.pallas_call(
        kernel,
        out_shape=out,
        in_specs=[spec] * count,
        out_specs=jax.tree.map(lambda _: spec, out),
        scratch_shapes=list(scratch),
        name=name,
    )


def shape(dims, kind):
    return jax.ShapeDtypeStruct(dims, kind)


def swap(value, axis, bit):
    size = lax.axis_size(axis)
    return lax.ppermute(value, axis, [(i, i ^ bit) for i in range(size)])


def body(
    fp_values,
    block_owner,
    block_obs,
    block_base,
    block_count,
    cover_index,
    cover_weight,
    spatial_cov,
    temporal_cov,
    obs_week,
    obs_error,
):
    n_tile = lax.axis_size("tile")
    n_blk = lax.axis_size("blk")
    cell_tile = spatial_cov.shape[1]
    slots, cells = fp_values.shape
    obs_rows = obs_error.shape[0]
    all_cells = cell_tile * n_tile
    width = obs_rows * n_blk // n_tile
    panel_width = min(PANEL_MAX, width)
    rows = slots + INDEX_ROWS
    error = obs_error.reshape(1, obs_rows)
    packed = call(pack_kernel, shape((rows, cells), BF16), 6, name="pack")(
        fp_values,
        block_obs.reshape(1, slots),
        block_base.reshape(1, slots),
        block_owner.reshape(1, slots),
        block_count.reshape(1, slots),
        error,
    )
    if direct(n_blk):
        order = list(range(n_blk - 1, 0, -1))
        got = {bit: swap(packed, "blk", bit) for bit in order}
        column = jnp.stack([packed] + [got[bit] for bit in range(1, n_blk)])
        got = {bit: swap(spatial_cov, "blk", bit) for bit in order}
        covs = [spatial_cov] + [got[bit] for bit in range(1, n_blk)]
    else:
        column = lax.all_gather(packed, "blk", axis=0)
        covs = [lax.all_gather(spatial_cov, "blk", axis=0, tiled=True)]
    raw = lax.all_gather(column, "tile", axis=0)
    product, head, head_error = call(
        functools.partial(product_kernel, slots, obs_rows),
        (
            shape((2 * obs_rows, cell_tile), BF16),
            shape((obs_rows, all_cells), BF16),
            shape((1, obs_rows), F32),
        ),
        3 + len(covs),
        scratch=[pltpu.VMEM((2 * obs_rows, all_cells), BF16)],
        name="product",
    )(raw, cover_index, cover_weight, *covs)
    if direct(n_tile):
        got = {bit: swap(product, "tile", bit) for bit in range(n_tile - 1, 0, -1)}
        products = [product] + [got[bit] for bit in range(1, n_tile)]
    else:
        products = [lax.all_gather(product, "tile", axis=0, tiled=True)]
    prints, week_cov = call(
        functools.partial(column_kernel, slots, obs_rows, panel_width),
        (
            shape((width, all_cells), BF16),
            shape((2 * obs_rows, panel_width + width), F32),
        ),
        5,
        name="column",
    )(raw, cover_index, cover_weight, obs_week.reshape(1, -1), temporal_cov)
    return call(
        functools.partial(final_kernel, obs_rows),
        (shape((obs_rows, panel_width), F32), shape((obs_rows, width), F32)),
        5 + len(products),
        scratch=[pltpu.VMEM((panel_width, panel_width), F32)],
        name="final",
    )(head, prints, week_cov, head_error, error, *products)


def solution(mesh):
    placed = (
        P(("grp", "blk", "tile"), None),
        P(("grp", "blk", "tile")),
        P(("grp", "blk", "tile")),
        P(("grp", "blk", "tile")),
        P(("grp", "blk", "tile")),
        P(),
        P(),
        P(("grp", "blk"), "tile"),
        P("grp", None),
        P("grp"),
        P(("grp", "blk")),
    )
    return jax.shard_map(
        body,
        mesh=mesh,
        in_specs=placed,
        out_specs=(P(("grp", "blk"), None), P(("grp", "blk"), "tile")),
        check_vma=False,
    )
```
